32 devices in a mesh: freq: 2 (over y), harm: 4 (over z), wall: 4 (over x, core).
Axes of the slice: x: 2, y: 2, z: 4, core: 2. Of those that a mesh axis runs over, the one named last changes fastest.
Arguments:
- sketch: bfloat16 [32, 1024, 128], P(('freq', 'harm'), 'wall'), parts along dimension 0, may hold values from -48 to 48
- inverse_blocks: bfloat16 [32, 1024, 1024], P(('freq', 'harm'), 'wall'), parts along dimension 0, may hold values from -0.1875 to 0.1875
- couple_up: bfloat16 [8, 1024, 1024], P('freq', 'wall'), parts along dimension 0, may hold values from -0.03125 to 0.03125
- couple_down: bfloat16 [8, 1024, 1024], P('freq', 'wall'), parts along dimension 0, may hold values from -0.03125 to 0.03125
- strip_harmonics: int32 [8], P('freq'), parts along dimension 0, may hold values from 0 to 3
Outputs:
- basis: float32 [32, 1024, 128], P(('freq', 'harm'), 'wall'), parts along dimension 0
- triangle: float32 [256, 128], P('freq'), parts along dimension 0
The draws below stay inside these ranges and needn't reach their ends.
There are 2 independent parts, one for each index of `freq`. The reference program is written for one: setup_inputs(seed, part) draws one part's arguments, and reference() takes and returns one part's arrays. A program takes and returns all parts, laid end to end along the dimension named above; each array names one. Nothing has to cross between parts.
Inputs may be any that keep to these rules, and one draw needn't show every extreme that they name: `strip_harmonics`: each entry one of 0 to 3; entries may repeat.
All inputs are finite; a program needn't handle non-finite values.
Results may differ from the reference program's by a relative error of at most 0.0045.
Values may be sent and summed in bfloat16 or wider, within the bound.
A program may use at most 64 MiB of HBM per device.

```python
import math
import jax
import jax.numpy as jnp
from jax import lax

ROWS = 1024
COLUMNS = 128
BAND = 4
SWEEPS = 3
HARMONICS = 16


def draw_sketch(key, part):
    scale_key = jax.random.fold_in(key, 7101)
    entry_key = jax.random.fold_in(key, 7102)
    levels = jax.random.uniform(scale_key, (HARMONICS, 1, 1), jnp.float32, 0.0, math.log(8.0))
    amplitude = jnp.exp(levels)
    entries = jnp.clip(jax.random.normal(entry_key, (HARMONICS, ROWS, COLUMNS), jnp.float32), -6.0, 6.0)
    return (entries * amplitude).astype(jnp.bfloat16)


def place_ends(drawn, rng, smallest, largest):
    index_at = [jax.random.randint(jax.random.fold_in(rng, axis), (), 0, length) for axis, length in enumerate(drawn.shape)]
    longest = drawn.shape.index(max(drawn.shape))
    next_to = index_at[:longest] + [(index_at[longest] + 1) % drawn.shape[longest]] + index_at[longest + 1:]
    return drawn.at[tuple(index_at)].set(smallest).at[tuple(next_to)].set(largest)


def level_of(own_key, dims, split, smallest, largest):
    gain = 1.0
    for axis_at, shards_of in split:
        heights = jax.random.uniform(jax.random.fold_in(jax.random.fold_in(own_key, 6), axis_at), (shards_of,), jnp.float32, smallest / len(split), largest / len(split))
        gain = gain * jnp.repeat(jnp.exp(heights), dims[axis_at] // shards_of).reshape((-1,) + (1,) * (len(dims) - 1 - axis_at))
    return gain


def gaussian(key, dims, width, reach, split=(), held_as=jnp.bfloat16):
    level = level_of(key, dims, split, -0.22, 0.18) if split else 1.0
    values = jax.random.normal(key, dims, jnp.float32) * width * level
    return jnp.minimum(jnp.maximum(values, -reach), reach).astype(held_as)


def setup_inputs(seed: int = 0, part: int = 0) -> dict:
    splits = jax.random.split(jax.random.key(seed), 6)
    part_keys = jax.random.split(jax.random.fold_in(splits[5], part), 6)
    sketch = draw_sketch(jax.random.fold_in(jax.random.fold_in(splits[5], part), 71), part)
    inverse_blocks = gaussian(part_keys[1], (HARMONICS, ROWS, ROWS), ROWS ** -0.5, 0.1875, ((0, 4), (1, 4)))
    couple_up = gaussian(part_keys[2], (BAND, ROWS, ROWS), (32 * ROWS) ** -0.5, 0.03125, ((1, 4),))
    couple_down = gaussian(part_keys[3], (BAND, ROWS, ROWS), (32 * ROWS) ** -0.5, 0.03125, ((1, 4),))
    strip_harmonics = place_ends(jax.random.randint(part_keys[4], (BAND,), 0, BAND), jax.random.fold_in(part_keys[4], 1), 0, BAND - 1).astype(jnp.int32)
    return {"sketch": sketch, "inverse_blocks": inverse_blocks, "couple_up": couple_up, "couple_down": couple_down, "strip_harmonics": strip_harmonics}


def reference(sketch, inverse_blocks, couple_up, couple_down, strip_harmonics):
    offsets = (strip_harmonics + 1).astype(jnp.int32)
    inverse_wide = inverse_blocks.astype(jnp.float32)
    up_wide = couple_up.astype(jnp.float32)
    down_wide = couple_down.astype(jnp.float32)
    sketch_wide = sketch.astype(jnp.float32)
    positions = jnp.arange(HARMONICS, dtype=jnp.int32)

    def apply_inverse(source):
        return jnp.einsum('hrc,hck->hrk', inverse_wide, source.astype(jnp.float32))
    state = apply_inverse(sketch).astype(jnp.bfloat16)
    sampled = None
    for sweep in range(SWEEPS):
        coupled = jnp.zeros((HARMONICS, ROWS, COLUMNS), jnp.float32)
        state_wide = state.astype(jnp.float32)
        for j in range(BAND):
            below = jnp.take(state_wide, (positions - offsets[j]) % HARMONICS, axis=0)
            above = jnp.take(state_wide, (positions + offsets[j]) % HARMONICS, axis=0)
            coupled = coupled + jnp.einsum('rc,hck->hrk', up_wide[j], below)
            coupled = coupled + jnp.einsum('rc,hck->hrk', down_wide[j], above)
        rhs = (sketch_wide - coupled).astype(jnp.bfloat16)
        result = apply_inverse(rhs)
        if sweep < SWEEPS - 1:
            state = result.astype(jnp.bfloat16)
        else:
            sampled = result
    flat = sampled.reshape(HARMONICS * ROWS, COLUMNS)
    count = HARMONICS * ROWS
    gram = jnp.dot(flat.T.astype(jnp.float32), flat.astype(jnp.float32), precision=lax.Precision.HIGHEST, preferred_element_type=jnp.float32) / count
    lower = jnp.linalg.cholesky(gram)
    basis = jax.scipy.linalg.solve_triangular(lower, flat.T, lower=True).T
    triangle = lower.T
    return (basis.reshape(HARMONICS, ROWS, COLUMNS), triangle)
```

```python
import functools

import jax
import jax.numpy as jnp
from jax import lax
from jax.experimental import pallas as pl
from jax.experimental.pallas import tpu as pltpu
from jax.sharding import PartitionSpec as P

BAND = 4
SWEEPS = 3
MESH = pl.DeviceIdType.MESH


def flip(index, bit):
    return index + bit - 2 * bit * (lax.div(index, bit) % 2)


def bits_of(count):
    return [1 << b for b in range(count.bit_length() - 1)]


def visit_order(count):
    order = []
    for i in range((count + 1) // 2):
        order += [i] if count - 1 - i == i else [i, count - 1 - i]
    return order


def sweep_kernel(
    walls, harms, strip, sketch, inverse, up, down, sampled, gram,
    pieces, inverse_v, couple_v, products, partial, halo_out, halo_in, gram_out, gram_in,
    load_sem, recv_sem, send_sem, halo_send, halo_recv, gram_send, gram_recv,
):
    count, rows, width = sketch.shape
    w = lax.axis_index("wall")
    z = lax.axis_index("harm")
    prev, following = (z + harms - 1) % harms, (z + 1) % harms
    wall_bits, harm_bits = bits_of(walls), bits_of(harms)
    order = visit_order(count)

    greet = [{"wall": flip(w, b)} for b in wall_bits]
    greet += [{"harm": flip(z, b)} for b in harm_bits]
    greet += [{"harm": prev}, {"harm": following}]
    barrier = pltpu.get_barrier_semaphore()

    loads = [
        pltpu.make_async_copy(inverse.at[h], inverse_v.at[h], load_sem.at[h]) for h in order
    ]
    loads += [
        pltpu.make_async_copy(up, couple_v.at[pl.ds(0, BAND)], load_sem.at[count]),
        pltpu.make_async_copy(down, couple_v.at[pl.ds(BAND, BAND)], load_sem.at[count + 1]),
    ]

    def block(g, h, m):
        source = w
        for b in wall_bits:
            if m & b:
                source = flip(source, b)
        return pieces.at[g, h, pl.ds(pl.multiple_of(source * rows, rows), rows)]

    own_copies = [
        pltpu.make_async_copy(sketch.at[h], block(0, h, 0), load_sem.at[count + 2 + h])
        for h in range(count)
    ]
    for copy in own_copies:
        copy.start()
    for peer in greet:
        pl.semaphore_signal(barrier, inc=1, device_id=peer, device_id_type=MESH)
    for copy in loads:
        copy.start()
    pl.semaphore_wait(barrier, len(greet))

    def hop(g, h, m, bit):
        return pltpu.make_async_remote_copy(
            src_ref=block(g, h, m), dst_ref=block(g, h, m),
            send_sem=send_sem.at[h, m + bit], recv_sem=recv_sem.at[g, h, m + bit],
            device_id={"wall": flip(w, bit)}, device_id_type=MESH,
        )

    def arrival(g, h, m):
        low = m & -m
        return pltpu.make_async_remote_copy(
            src_ref=block(g, h, m), dst_ref=block(g, h, m),
            send_sem=send_sem.at[h, m], recv_sem=recv_sem.at[g, h, m],
            device_id={"wall": flip(w, low)}, device_id_type=MESH,
        )

    def send_own(g, h):
        for bit in reversed(wall_bits):
            hop(g, h, 0, bit).start()

    def collect(g, h):
        for m in sorted(range(1, walls), key=lambda m: -(m & -m)):
            arrival(g, h, m).wait_recv()
            for bit in reversed(wall_bits):
                if bit < (m & -m):
                    hop(g, h, m, bit).start()

    def settle(g, h):
        for m in range(1, walls):
            arrival(g, h, m).wait_send()

    def apply_inverse(g, h):
        return jnp.dot(inverse_v[h], pieces[g, h], preferred_element_type=jnp.float32)

    def store_own(g, h, value):
        pieces[g, h, pl.ds(pl.multiple_of(w * rows, rows), rows), :] = value

    for h in order:
        own_copies[h].wait()
        send_own(0, h)

    blank = jnp.zeros((rows, width), jnp.float32)

    @pl.loop(0, 2 * BAND)
    def _(j):
        for slot in range(BAND):
            products[j, slot] = blank
            products[j, count + BAND + slot] = blank

    for i, h in enumerate(order):
        collect(0, h)
        loads[i].wait()
        state = apply_inverse(0, h).astype(jnp.bfloat16)
        settle(0, h)
        store_own(1, h, state)
        send_own(1, h)
    loads[count].wait()
    loads[count + 1].wait()

    offsets = [strip[j] + 1 for j in range(BAND)]

    def halo(s, side, i):
        return pltpu.make_async_remote_copy(
            src_ref=halo_out.at[s, side, i], dst_ref=halo_in.at[s, side, i],
            send_sem=halo_send.at[side, i], recv_sem=halo_recv.at[s, side, i],
            device_id={"harm": prev if side == 0 else following}, device_id_type=MESH,
        )

    def from_below(t):
        total = products[0, t - offsets[0] + BAND]
        for j in range(1, BAND):
            total = total + products[j, t - offsets[j] + BAND]
        return total

    def from_above(t):
        total = products[BAND, t + offsets[0] + BAND]
        for j in range(1, BAND):
            total = total + products[BAND + j, t + offsets[j] + BAND]
        return total

    slots = []
    for i in range(BAND):
        slots.append((1, i, {count + i - o for o in range(1, BAND + 1)}))
        slots.append((0, BAND - 1 - i, {o - 1 - i for o in range(1, BAND + 1)}))
    slots = [(side, i, {h for h in need if 0 <= h < count}) for side, i, need in slots]

    for s in range(SWEEPS):
        g_state, g_rhs = 1 + 2 * s, 2 + 2 * s
        done, sent = set(), set()
        for h in order:
            collect(g_state, h)

            @pl.loop(0, 2 * BAND)
            def _(j):
                products[j, h + BAND] = jnp.dot(
                    couple_v[j], pieces[g_state, h], preferred_element_type=jnp.float32
                )

            done.add(h)
            for side, i, need in slots:
                if (side, i) not in sent and need <= done:
                    sent.add((side, i))
                    value = from_above(i - BAND) if side == 0 else from_below(count + i)
                    halo_out[s, side, i] = value.astype(jnp.bfloat16)
                    halo(s, side, i).start()
        for h in order:
            settle(g_state, h)
            own = pieces[0, h, pl.ds(pl.multiple_of(w * rows, rows), rows), :]
            partial[h] = own.astype(jnp.float32) - (from_below(h) + from_above(h))
        for h in order:
            rhs = partial[h]
            if h < BAND:
                halo(s, 1, h).wait_recv()
                rhs = rhs - halo_in[s, 1, h].astype(jnp.float32)
            if h >= count - BAND:
                i = h - count + BAND
                halo(s, 0, i).wait_recv()
                rhs = rhs - halo_in[s, 0, i].astype(jnp.float32)
            store_own(g_rhs, h, rhs.astype(jnp.bfloat16))
            send_own(g_rhs, h)
        for side in range(2):
            for i in range(BAND):
                halo(s, side, i).wait_send()
        total = jnp.zeros((width, width), jnp.float32)
        for h in order:
            collect(g_rhs, h)
            result = apply_inverse(g_rhs, h)
            settle(g_rhs, h)
            if s < SWEEPS - 1:
                store_own(g_rhs + 1, h, result.astype(jnp.bfloat16))
                send_own(g_rhs + 1, h)
            else:
                sampled[h] = result
                total = total + lax.dot_general(
                    result, result, (((0,), (0,)), ((), ())),
                    precision=lax.Precision.HIGHEST, preferred_element_type=jnp.float32,
                )

    stages = [("wall", flip(w, b)) for b in wall_bits] + [("harm", flip(z, b)) for b in harm_bits]
    for stage, (axis, peer) in enumerate(stages):
        gram_out[stage] = total
        swap = pltpu.make_async_remote_copy(
            src_ref=gram_out.at[stage], dst_ref=gram_in.at[stage],
            send_sem=gram_send.at[stage], recv_sem=gram_recv.at[stage],
            device_id={axis: peer}, device_id_type=MESH,
        )
        swap.start()
        swap.wait()
        total = total + gram_in[stage]
    gram[...] = total / (harms * walls * count * rows)


def factor_kernel(sampled, gram, basis, triangle, work, inverse_lower):
    count, rows, width = sampled.shape
    row_at = lax.broadcasted_iota(jnp.int32, (width, width), 0)
    col_at = lax.broadcasted_iota(jnp.int32, (width, width), 1)
    work[...] = gram[...]
    inverse_lower[...] = jnp.where(row_at == col_at, 1.0, 0.0)

    @pl.loop(0, width)
    def _(k):
        a = work[...]
        x = inverse_lower[...]
        row = work[pl.ds(k, 1), :]
        x_row = inverse_lower[pl.ds(k, 1), :]
        column = jnp.sum(jnp.where(col_at == k, a, 0.0), axis=1, keepdims=True)
        pivot = jnp.sum(jnp.where(col_at[:1] == k, row, 0.0), axis=1, keepdims=True)
        unit = lax.rsqrt(pivot)
        factor = jnp.where(row_at[:, :1] > k, column / pivot, 0.0)
        here = row_at == k
        work[...] = jnp.where(here, row * unit, a - factor * row)
        inverse_lower[...] = jnp.where(here, x_row * unit, x - factor * x_row)

    triangle[...] = jnp.where(row_at <= col_at, work[...], 0.0)
    for h in range(count):
        basis[h] = lax.dot_general(
            sampled[h], inverse_lower[...], (((1,), (1,)), ((), ())),
            precision=lax.Precision.HIGHEST, preferred_element_type=jnp.float32,
        )


def body(walls, harms, sketch, inverse_blocks, couple_up, couple_down, strip_harmonics):
    count, rows, width = sketch.shape
    size = rows * walls
    wall_hops, stages = len(bits_of(walls)), len(bits_of(walls)) + len(bits_of(harms))
    gathers = 1 + 2 * SWEEPS
    vmem = pl.BlockSpec(memory_space=pltpu.VMEM)
    anywhere = pl.BlockSpec(memory_space=pl.ANY)
    sampled, gram = pl.pallas_call(
        functools.partial(sweep_kernel, walls, harms),
        out_shape=(
            jax.ShapeDtypeStruct((count, rows, width), jnp.float32),
            jax.ShapeDtypeStruct((width, width), jnp.float32),
        ),
        in_specs=[pl.BlockSpec(memory_space=pltpu.SMEM)] + [anywhere] * 4,
        out_specs=(vmem, vmem),
        scratch_shapes=[
            pltpu.VMEM((gathers, count, size, width), jnp.bfloat16),
            pltpu.VMEM((count, rows, size), jnp.bfloat16),
            pltpu.VMEM((2 * BAND, rows, size), jnp.bfloat16),
            pltpu.VMEM((2 * BAND, count + 2 * BAND, rows, width), jnp.float32),
            pltpu.VMEM((count, rows, width), jnp.float32),
            pltpu.VMEM((SWEEPS, 2, BAND, rows, width), jnp.bfloat16),
            pltpu.VMEM((SWEEPS, 2, BAND, rows, width), jnp.bfloat16),
            pltpu.VMEM((stages, width, width), jnp.float32),
            pltpu.VMEM((stages, width, width), jnp.float32),
            pltpu.SemaphoreType.DMA((2 * count + 2,)),
            pltpu.SemaphoreType.DMA((gathers, count, walls)),
            pltpu.SemaphoreType.DMA((count, walls)),
            pltpu.SemaphoreType.DMA((2, BAND)),
            pltpu.SemaphoreType.DMA((SWEEPS, 2, BAND)),
            pltpu.SemaphoreType.DMA((stages,)),
            pltpu.SemaphoreType.DMA((stages,)),
        ],
        compiler_params=pltpu.CompilerParams(
            collective_id=0, has_side_effects=True, vmem_limit_bytes=48 * 1024 * 1024
        ),
        name="sweeps",
    )(strip_harmonics, sketch, inverse_blocks, couple_up, couple_down)
    return pl.pallas_call(
        factor_kernel,
        out_shape=(
            jax.ShapeDtypeStruct((count, rows, width), jnp.float32),
            jax.ShapeDtypeStruct((width, width), jnp.float32),
        ),
        in_specs=[vmem, vmem],
        out_specs=(vmem, vmem),
        scratch_shapes=[pltpu.VMEM((width, width), jnp.float32)] * 2,
        name="factor",
    )(sampled, gram)


def solution(mesh):
    return jax.shard_map(
        functools.partial(body, mesh.shape["wall"], mesh.shape["harm"]),
        mesh=mesh,
        in_specs=(
            P(("freq", "harm"), "wall", None),
            P(("freq", "harm"), "wall", None),
            P("freq", "wall", None),
            P("freq", "wall", None),
            P("freq"),
        ),
        out_specs=(P(("freq", "harm"), "wall", None), P("freq", None)),
        check_vma=False,
    )
```

```python
import functools

import jax
import jax.numpy as jnp
from jax import lax
from jax.experimental import pallas as pl
from jax.experimental.pallas import tpu as pltpu
from jax.sharding import PartitionSpec as P

BAND = 4
SWEEPS = 3
MESH = pl.DeviceIdType.MESH


def flip(index, bit):
    return index + bit - 2 * bit * (lax.div(index, bit) % 2)


def bits_of(count):
    return [1 << b for b in range(count.bit_length() - 1)]


def visit_order(count):
    order = []
    for i in range((count + 1) // 2):
        order += [i] if count - 1 - i == i else [i, count - 1 - i]
    return order


def sweep_kernel(
    walls, harms, strip, sketch, inverse, up, down, sampled, gram,
    pieces, inverse_v, couple_v, products, partial, halo_out, halo_in,
    whole, summed, gathered, gram_out, gram_in,
    load_sem, recv_sem, send_sem, halo_send, halo_recv, gram_send, gram_recv,
):
    count, rows, width = sketch.shape
    w = lax.axis_index("wall")
    z = lax.axis_index("harm")
    prev, following = (z + harms - 1) % harms, (z + 1) % harms
    wall_bits, harm_bits = bits_of(walls), bits_of(harms)
    order = visit_order(count)

    near = min(4, harms)
    butterfly = [("wall", flip(w, b)) for b in wall_bits if b > 1]
    butterfly += [("harm", flip(z, b)) for b in harm_bits if b >= near]
    greet = [{"wall": flip(w, b)} for b in wall_bits]
    greet += [{"harm": flip(z, b)} for b in harm_bits if b >= near]
    greet += [{"harm": z - z % near + (z % near + d) % near} for d in range(1, near)]
    greet += [{"harm": prev}, {"harm": following}]
    barrier = pltpu.get_barrier_semaphore()

    loads = [
        pltpu.make_async_copy(inverse.at[h], inverse_v.at[h], load_sem.at[h]) for h in order
    ]
    loads += [
        pltpu.make_async_copy(up, couple_v.at[pl.ds(0, BAND)], load_sem.at[count]),
        pltpu.make_async_copy(down, couple_v.at[pl.ds(BAND, BAND)], load_sem.at[count + 1]),
    ]

    def block(g, h, m):
        source = w
        for b in wall_bits:
            if m & b:
                source = flip(source, b)
        return pieces.at[g, h, pl.ds(pl.multiple_of(source * rows, rows), rows)]

    own_copies = [
        pltpu.make_async_copy(sketch.at[h], block(0, h, 0), load_sem.at[count + 2 + h])
        for h in range(count)
    ]
    for copy in own_copies:
        copy.start()
    for peer in greet:
        pl.semaphore_signal(barrier, inc=1, device_id=peer, device_id_type=MESH)
    for copy in loads:
        copy.start()
    pl.semaphore_wait(barrier, len(greet))

    def hop(g, h, m, bit):
        return pltpu.make_async_remote_copy(
            src_ref=block(g, h, m), dst_ref=block(g, h, m),
            send_sem=send_sem.at[h, m + bit], recv_sem=recv_sem.at[g, h, m + bit],
            device_id={"wall": flip(w, bit)}, device_id_type=MESH,
        )

    def arrival(g, h, m):
        low = m & -m
        return pltpu.make_async_remote_copy(
            src_ref=block(g, h, m), dst_ref=block(g, h, m),
            send_sem=send_sem.at[h, m], recv_sem=recv_sem.at[g, h, m],
            device_id={"wall": flip(w, low)}, device_id_type=MESH,
        )

    def send_own(g, h):
        for bit in reversed(wall_bits):
            hop(g, h, 0, bit).start()

    def collect(g, h):
        for m in sorted(range(1, walls), key=lambda m: -(m & -m)):
            arrival(g, h, m).wait_recv()
            for bit in reversed(wall_bits):
                if bit < (m & -m):
                    hop(g, h, m, bit).start()

    def settle(g, h):
        for m in range(1, walls):
            arrival(g, h, m).wait_send()

    def apply_inverse(g, h):
        return jnp.dot(inverse_v[h], pieces[g, h], preferred_element_type=jnp.float32)

    def store_own(g, h, value):
        pieces[g, h, pl.ds(pl.multiple_of(w * rows, rows), rows), :] = value

    for h in order:
        own_copies[h].wait()
        send_own(0, h)

    blank = jnp.zeros((rows, width), jnp.float32)

    @pl.loop(0, 2 * BAND)
    def _(j):
        for slot in range(BAND):
            products[j, slot] = blank
            products[j, count + BAND + slot] = blank

    for i, h in enumerate(order):
        collect(0, h)
        loads[i].wait()
        state = apply_inverse(0, h).astype(jnp.bfloat16)
        settle(0, h)
        store_own(1, h, state)
        send_own(1, h)
    loads[count].wait()
    loads[count + 1].wait()

    offsets = [strip[j] + 1 for j in range(BAND)]

    def halo(s, side, i):
        return pltpu.make_async_remote_copy(
            src_ref=halo_out.at[s, side, i], dst_ref=halo_in.at[s, side, i],
            send_sem=halo_send.at[side, i], recv_sem=halo_recv.at[s, side, i],
            device_id={"harm": prev if side == 0 else following}, device_id_type=MESH,
        )

    def from_below(t):
        total = products[0, t - offsets[0] + BAND]
        for j in range(1, BAND):
            total = total + products[j, t - offsets[j] + BAND]
        return total

    def from_above(t):
        total = products[BAND, t + offsets[0] + BAND]
        for j in range(1, BAND):
            total = total + products[BAND + j, t + offsets[j] + BAND]
        return total

    slots = []
    for i in range(BAND):
        slots.append((1, i, {count + i - o for o in range(1, BAND + 1)}))
        slots.append((0, BAND - 1 - i, {o - 1 - i for o in range(1, BAND + 1)}))
    slots = [(side, i, {h for h in need if 0 <= h < count}) for side, i, need in slots]

    for s in range(SWEEPS):
        g_state, g_rhs = 1 + 2 * s, 2 + 2 * s
        done, sent = set(), set()
        for start in range(0, count, 2):
            group = order[start : start + 2]
            for h in group:
                collect(g_state, h)

            @pl.loop(0, 2 * BAND)
            def _(j):
                state = jnp.concatenate([pieces[g_state, h] for h in group], axis=1)
                both = jnp.dot(couple_v[j], state, preferred_element_type=jnp.float32)
                for at, h in enumerate(group):
                    products[j, h + BAND] = both[:, at * width : (at + 1) * width]

            done |= set(group)
            for side, i, need in slots:
                if (side, i) not in sent and need <= done:
                    sent.add((side, i))
                    value = from_above(i - BAND) if side == 0 else from_below(count + i)
                    halo_out[s, side, i] = value.astype(jnp.bfloat16)
                    halo(s, side, i).start()
        for h in order:
            settle(g_state, h)
            own = pieces[0, h, pl.ds(pl.multiple_of(w * rows, rows), rows), :]
            partial[h] = own.astype(jnp.float32) - (from_below(h) + from_above(h))
        for h in order:
            rhs = partial[h]
            if h < BAND:
                halo(s, 1, h).wait_recv()
                rhs = rhs - halo_in[s, 1, h].astype(jnp.float32)
            if h >= count - BAND:
                i = h - count + BAND
                halo(s, 0, i).wait_recv()
                rhs = rhs - halo_in[s, 0, i].astype(jnp.float32)
            store_own(g_rhs, h, rhs.astype(jnp.bfloat16))
            send_own(g_rhs, h)
        for side in range(2):
            for i in range(BAND):
                halo(s, side, i).wait_send()
        total = jnp.zeros((width, width), jnp.float32)
        for h in order:
            collect(g_rhs, h)
            result = apply_inverse(g_rhs, h)
            settle(g_rhs, h)
            if s < SWEEPS - 1:
                store_own(g_rhs + 1, h, result.astype(jnp.bfloat16))
                send_own(g_rhs + 1, h)
            else:
                sampled[h] = result
                total = total + lax.dot_general(
                    result, result, (((0,), (0,)), ((), ())),
                    precision=lax.Precision.HIGHEST, preferred_element_type=jnp.float32,
                )

    part = width // 2
    mine, theirs = (w % 2) * part, (1 - w % 2) * part

    def swap(stage, source, target, peer):
        copy = pltpu.make_async_remote_copy(
            src_ref=source, dst_ref=target, send_sem=gram_send.at[stage],
            recv_sem=gram_recv.at[stage], device_id=peer, device_id_type=MESH,
        )
        copy.start()
        return copy

    whole[...] = total
    swap(
        0, whole.at[pl.ds(pl.multiple_of(theirs, part), part)], gram_in.at[0], {"wall": flip(w, 1)}
    ).wait()
    half = whole[pl.ds(pl.multiple_of(mine, part), part), :] + gram_in[0]
    stage = 1
    for axis, peer in butterfly:
        gram_out[stage] = half
        swap(stage, gram_out.at[stage], gram_in.at[stage], {axis: peer}).wait()
        half = half + gram_in[stage]
        stage += 1
    me = z % near
    gathered[me] = half
    copies = [
        swap(stage + d - 1, gathered.at[me], gathered.at[me], {"harm": z - me + (me + d) % near})
        for d in range(1, near)
    ]
    for copy in copies:
        copy.wait()
    half = gathered[0]
    for d in range(1, near):
        half = half + gathered[d]
    stage += near - 1
    half = half / (harms * walls * count * rows)
    place = pl.ds(pl.multiple_of(mine, part), part)
    summed[place, :] = half
    swap(stage, summed.at[place], summed.at[place], {"wall": flip(w, 1)}).wait()
    gram[...] = summed[...]


def factor_kernel(sampled, gram, basis, triangle, work, inverse_lower):
    count, rows, width = sampled.shape
    panel = 8
    row_at = lax.broadcasted_iota(jnp.int32, (width, width), 0)
    col_at = lax.broadcasted_iota(jnp.int32, (width, width), 1)
    at = lax.broadcasted_iota(jnp.int32, (panel, width), 0)
    work[...] = gram[...]
    inverse_lower[...] = jnp.where(row_at == col_at, 1.0, 0.0)

    def spread(value, i):
        return jnp.broadcast_to(value[i : i + 1, :], (panel, width))

    for low in range(0, width, panel):
        a = work[low : low + panel, :]
        x = inverse_lower[low : low + panel, :]
        columns = [
            jnp.broadcast_to(a[:, low + i : low + i + 1], (panel, width)) for i in range(panel)
        ]
        pivots = jnp.ones((panel, width), jnp.float32)
        for i in range(panel):
            pivot = spread(columns[i], i)
            pivots = jnp.where(at == i, pivot, pivots)
            factor = jnp.where(at > i, columns[i] * (1.0 / pivot), 0.0)
            for m in range(i + 1, panel):
                columns[m] = columns[m] - factor * spread(columns[m], i)
            a = a - factor * spread(a, i)
            x = x - factor * spread(x, i)
        unit = lax.rsqrt(pivots)
        a, x = a * unit, x * unit
        work[low : low + panel, :] = a
        inverse_lower[low : low + panel, :] = x
        if low + panel < width:
            change = lax.dot_general(
                a, jnp.concatenate([a, x], axis=1), (((0,), (0,)), ((), ())),
                precision=lax.Precision.HIGHEST, preferred_element_type=jnp.float32,
            )
            below = low + panel
            work[below:, :] = work[below:, :] - change[below:, :width]
            inverse_lower[below:, :] = inverse_lower[below:, :] - change[below:, width:]

    triangle[...] = jnp.where(row_at <= col_at, work[...], 0.0)
    for h in range(count):
        basis[h] = lax.dot_general(
            sampled[h], inverse_lower[...], (((1,), (1,)), ((), ())),
            precision=lax.Precision.HIGHEST, preferred_element_type=jnp.float32,
        )


def body(walls, harms, sketch, inverse_blocks, couple_up, couple_down, strip_harmonics):
    count, rows, width = sketch.shape
    size = rows * walls
    near = min(4, harms)
    stages = len(bits_of(walls)) + len(bits_of(harms // near)) + near
    gathers = 1 + 2 * SWEEPS
    vmem = pl.BlockSpec(memory_space=pltpu.VMEM)
    anywhere = pl.BlockSpec(memory_space=pl.ANY)
    sampled, gram = pl.pallas_call(
        functools.partial(sweep_kernel, walls, harms),
        out_shape=(
            jax.ShapeDtypeStruct((count, rows, width), jnp.float32),
            jax.ShapeDtypeStruct((width, width), jnp.float32),
        ),
        in_specs=[pl.BlockSpec(memory_space=pltpu.SMEM)] + [anywhere] * 4,
        out_specs=(vmem, vmem),
        scratch_shapes=[
            pltpu.VMEM((gathers, count, size, width), jnp.bfloat16),
            pltpu.VMEM((count, rows, size), jnp.bfloat16),
            pltpu.VMEM((2 * BAND, rows, size), jnp.bfloat16),
            pltpu.VMEM((2 * BAND, count + 2 * BAND, rows, width), jnp.float32),
            pltpu.VMEM((count, rows, width), jnp.float32),
            pltpu.VMEM((SWEEPS, 2, BAND, rows, width), jnp.bfloat16),
            pltpu.VMEM((SWEEPS, 2, BAND, rows, width), jnp.bfloat16),
            pltpu.VMEM((width, width), jnp.float32),
            pltpu.VMEM((width, width), jnp.float32),
            pltpu.VMEM((near, width // 2, width), jnp.float32),
            pltpu.VMEM((stages, width // 2, width), jnp.float32),
            pltpu.VMEM((stages, width // 2, width), jnp.float32),
            pltpu.SemaphoreType.DMA((2 * count + 2,)),
            pltpu.SemaphoreType.DMA((gathers, count, walls)),
            pltpu.SemaphoreType.DMA((count, walls)),
            pltpu.SemaphoreType.DMA((2, BAND)),
            pltpu.SemaphoreType.DMA((SWEEPS, 2, BAND)),
            pltpu.SemaphoreType.DMA((stages,)),
            pltpu.SemaphoreType.DMA((stages,)),
        ],
        compiler_params=pltpu.CompilerParams(
            collective_id=0, has_side_effects=True, vmem_limit_bytes=67043328
        ),
        name="sweeps",
    )(strip_harmonics, sketch, inverse_blocks, couple_up, couple_down)
    return pl.pallas_call(
        factor_kernel,
        out_shape=(
            jax.ShapeDtypeStruct((count, rows, width), jnp.float32),
            jax.ShapeDtypeStruct((width, width), jnp.float32),
        ),
        in_specs=[vmem, vmem],
        out_specs=(vmem, vmem),
        scratch_shapes=[pltpu.VMEM((width, width), jnp.float32)] * 2,
        name="factor",
    )(sampled, gram)


def solution(mesh):
    return jax.shard_map(
        functools.partial(body, mesh.shape["wall"], mesh.shape["harm"]),
        mesh=mesh,
        in_specs=(
            P(("freq", "harm"), "wall", None),
            P(("freq", "harm"), "wall", None),
            P("freq", "wall", None),
            P("freq", "wall", None),
            P("freq"),
        ),
        out_specs=(P(("freq", "harm"), "wall", None), P("freq", None)),
        check_vma=False,
    )
```

```python
import functools

import jax
import jax.numpy as jnp
from jax import lax
from jax.experimental import pallas as pl
from jax.experimental.pallas import tpu as pltpu
from jax.sharding import PartitionSpec as P

BAND = 4
SWEEPS = 3
MESH = pl.DeviceIdType.MESH


def flip(index, bit):
    return index + bit - 2 * bit * (lax.div(index, bit) % 2)


def bits_of(count):
    return [1 << b for b in range(count.bit_length() - 1)]


def visit_order(count):
    order = []
    for i in range((count + 1) // 2):
        order += [i] if count - 1 - i == i else [i, count - 1 - i]
    return order


def sweep_kernel(
    walls, harms, strip, sketch, inverse, up, down, sampled, gram,
    pieces, inverse_v, couple_v, products, partial, halo_out, halo_in,
    whole, summed, gathered, gram_out, gram_in,
    load_sem, recv_sem, send_sem, halo_send, halo_recv, gram_send, gram_recv,
):
    count, rows, width = sketch.shape
    w = lax.axis_index("wall")
    z = lax.axis_index("harm")
    prev, following = (z + harms - 1) % harms, (z + 1) % harms
    wall_bits, harm_bits = bits_of(walls), bits_of(harms)
    order = visit_order(count)

    near = min(4, harms)
    butterfly = [("wall", flip(w, b)) for b in wall_bits if b > 1]
    butterfly += [("harm", flip(z, b)) for b in harm_bits if b >= near]
    greet = [{"wall": flip(w, b)} for b in wall_bits]
    greet += [{"harm": flip(z, b)} for b in harm_bits if b >= near]
    greet += [{"harm": z - z % near + (z % near + d) % near} for d in range(1, near)]
    greet += [{"harm": prev}, {"harm": following}]
    barrier = pltpu.get_barrier_semaphore()

    loads = [
        pltpu.make_async_copy(inverse.at[h], inverse_v.at[h], load_sem.at[h]) for h in order
    ]
    loads += [
        pltpu.make_async_copy(up, couple_v.at[pl.ds(0, BAND)], load_sem.at[count]),
        pltpu.make_async_copy(down, couple_v.at[pl.ds(BAND, BAND)], load_sem.at[count + 1]),
    ]

    def block(g, h, m):
        source = w
        for b in wall_bits:
            if m & b:
                source = flip(source, b)
        return pieces.at[g, h, pl.ds(pl.multiple_of(source * rows, rows), rows)]

    own_copies = [
        pltpu.make_async_copy(sketch.at[h], block(0, h, 0), load_sem.at[count + 2 + h])
        for h in range(count)
    ]
    for copy in own_copies:
        copy.start()
    for peer in greet:
        pl.semaphore_signal(barrier, inc=1, device_id=peer, device_id_type=MESH)
    for copy in loads:
        copy.start()
    pl.semaphore_wait(barrier, len(greet))

    def hop(g, h, m, bit):
        return pltpu.make_async_remote_copy(
            src_ref=block(g, h, m), dst_ref=block(g, h, m),
            send_sem=send_sem.at[h, m + bit], recv_sem=recv_sem.at[g, h, m + bit],
            device_id={"wall": flip(w, bit)}, device_id_type=MESH,
        )

    def arrival(g, h, m):
        low = m & -m
        return pltpu.make_async_remote_copy(
            src_ref=block(g, h, m), dst_ref=block(g, h, m),
            send_sem=send_sem.at[h, m], recv_sem=recv_sem.at[g, h, m],
            device_id={"wall": flip(w, low)}, device_id_type=MESH,
        )

    def send_own(g, h):
        for bit in reversed(wall_bits):
            hop(g, h, 0, bit).start()

    def relay(g, h):
        for m in sorted(range(2, walls, 2), key=lambda m: -(m & -m)):
            arrival(g, h, m).wait_recv()
            for bit in reversed(wall_bits):
                if bit < (m & -m):
                    hop(g, h, m, bit).start()

    def finish(g, h):
        for m in range(1, walls, 2):
            arrival(g, h, m).wait_recv()

    def collect(g, h):
        relay(g, h)
        finish(g, h)

    def settle(g, h):
        for m in range(1, walls):
            arrival(g, h, m).wait_send()

    def apply_inverse(g, h):
        return jnp.dot(inverse_v[h], pieces[g, h], preferred_element_type=jnp.float32)

    def store_own(g, h, value):
        pieces[g, h, pl.ds(pl.multiple_of(w * rows, rows), rows), :] = value

    for h in order:
        own_copies[h].wait()
        send_own(0, h)

    blank = jnp.zeros((rows, width), jnp.float32)

    @pl.loop(0, 2 * BAND)
    def _(j):
        for slot in range(BAND):
            products[j, slot] = blank
            products[j, count + BAND + slot] = blank

    for i, h in enumerate(order):
        collect(0, h)
        loads[i].wait()
        state = apply_inverse(0, h).astype(jnp.bfloat16)
        settle(0, h)
        store_own(1, h, state)
        send_own(1, h)
    loads[count].wait()
    loads[count + 1].wait()

    offsets = [strip[j] + 1 for j in range(BAND)]

    def halo(s, side, i):
        return pltpu.make_async_remote_copy(
            src_ref=halo_out.at[s, side, i], dst_ref=halo_in.at[s, side, i],
            send_sem=halo_send.at[side, i], recv_sem=halo_recv.at[s, side, i],
            device_id={"harm": prev if side == 0 else following}, device_id_type=MESH,
        )

    def from_below(t):
        total = products[0, t - offsets[0] + BAND]
        for j in range(1, BAND):
            total = total + products[j, t - offsets[j] + BAND]
        return total

    def from_above(t):
        total = products[BAND, t + offsets[0] + BAND]
        for j in range(1, BAND):
            total = total + products[BAND + j, t + offsets[j] + BAND]
        return total

    slots = []
    for i in range(BAND):
        slots.append((1, i, {count + i - o for o in range(1, BAND + 1)}))
        slots.append((0, BAND - 1 - i, {o - 1 - i for o in range(1, BAND + 1)}))
    slots = [(side, i, {h for h in need if 0 <= h < count}) for side, i, need in slots]

    for s in range(SWEEPS):
        g_state, g_rhs = 1 + 2 * s, 2 + 2 * s
        done, sent = set(), set()
        for start in range(0, count, 2):
            group, later = order[start : start + 2], order[start + 2 : start + 4]
            for h in group:
                if start == 0:
                    relay(g_state, h)
            for h in group:
                finish(g_state, h)

            def couple(j):
                state = jnp.concatenate([pieces[g_state, h] for h in group], axis=1)
                both = jnp.dot(couple_v[j], state, preferred_element_type=jnp.float32)
                for at, h in enumerate(group):
                    products[j, h + BAND] = both[:, at * width : (at + 1) * width]

            pl.loop(0, BAND, unroll=BAND)(couple)
            for h in later:
                relay(g_state, h)
            pl.loop(BAND, 2 * BAND, unroll=BAND)(couple)
            done |= set(group)
            for side, i, need in slots:
                if (side, i) not in sent and need <= done:
                    sent.add((side, i))
                    value = from_above(i - BAND) if side == 0 else from_below(count + i)
                    halo_out[s, side, i] = value.astype(jnp.bfloat16)
                    halo(s, side, i).start()
        for h in order:
            settle(g_state, h)
            own = pieces[0, h, pl.ds(pl.multiple_of(w * rows, rows), rows), :]
            partial[h] = own.astype(jnp.float32) - (from_below(h) + from_above(h))
        for h in order:
            rhs = partial[h]
            if h < BAND:
                halo(s, 1, h).wait_recv()
                rhs = rhs - halo_in[s, 1, h].astype(jnp.float32)
            if h >= count - BAND:
                i = h - count + BAND
                halo(s, 0, i).wait_recv()
                rhs = rhs - halo_in[s, 0, i].astype(jnp.float32)
            store_own(g_rhs, h, rhs.astype(jnp.bfloat16))
            send_own(g_rhs, h)
        for side in range(2):
            for i in range(BAND):
                halo(s, side, i).wait_send()
        total = jnp.zeros((width, width), jnp.float32)
        for h in order:
            collect(g_rhs, h)
            result = apply_inverse(g_rhs, h)
            settle(g_rhs, h)
            if s < SWEEPS - 1:
                store_own(g_rhs + 1, h, result.astype(jnp.bfloat16))
                send_own(g_rhs + 1, h)
            else:
                sampled[h] = result
                total = total + lax.dot_general(
                    result, result, (((0,), (0,)), ((), ())),
                    precision=lax.Precision.HIGHEST, preferred_element_type=jnp.float32,
                )

    part = width // 2
    mine, theirs = (w % 2) * part, (1 - w % 2) * part

    def swap(stage, source, target, peer):
        copy = pltpu.make_async_remote_copy(
            src_ref=source, dst_ref=target, send_sem=gram_send.at[stage],
            recv_sem=gram_recv.at[stage], device_id=peer, device_id_type=MESH,
        )
        copy.start()
        return copy

    whole[...] = total
    swap(
        0, whole.at[pl.ds(pl.multiple_of(theirs, part), part)], gram_in.at[0], {"wall": flip(w, 1)}
    ).wait()
    half = whole[pl.ds(pl.multiple_of(mine, part), part), :] + gram_in[0]
    stage = 1
    for axis, peer in butterfly:
        gram_out[stage] = half
        swap(stage, gram_out.at[stage], gram_in.at[stage], {axis: peer}).wait()
        half = half + gram_in[stage]
        stage += 1
    me = z % near
    gathered[me] = half
    copies = [
        swap(stage + d - 1, gathered.at[me], gathered.at[me], {"harm": z - me + (me + d) % near})
        for d in range(1, near)
    ]
    for copy in copies:
        copy.wait()
    half = gathered[0]
    for d in range(1, near):
        half = half + gathered[d]
    stage += near - 1
    half = half / (harms * walls * count * rows)
    place = pl.ds(pl.multiple_of(mine, part), part)
    summed[place, :] = half
    swap(stage, summed.at[place], summed.at[place], {"wall": flip(w, 1)}).wait()
    gram[...] = summed[...]


def factor_kernel(sampled, gram, basis, triangle, work, inverse_lower):
    count, rows, width = sampled.shape
    panel = 8
    row_at = lax.broadcasted_iota(jnp.int32, (width, width), 0)
    col_at = lax.broadcasted_iota(jnp.int32, (width, width), 1)
    at = lax.broadcasted_iota(jnp.int32, (panel, width), 0)
    work[...] = gram[...]
    inverse_lower[...] = jnp.where(row_at == col_at, 1.0, 0.0)

    def spread(value, i):
        return jnp.broadcast_to(value[i : i + 1, :], (panel, width))

    for low in range(0, width, panel):
        a = work[low : low + panel, :]
        x = inverse_lower[low : low + panel, :]
        columns = [
            jnp.broadcast_to(a[:, low + i : low + i + 1], (panel, width)) for i in range(panel)
        ]
        pivots = jnp.ones((panel, width), jnp.float32)
        for i in range(panel):
            pivot = spread(columns[i], i)
            pivots = jnp.where(at == i, pivot, pivots)
            factor = jnp.where(at > i, columns[i] * (1.0 / pivot), 0.0)
            for m in range(i + 1, panel):
                columns[m] = columns[m] - factor * spread(columns[m], i)
            a = a - factor * spread(a, i)
            x = x - factor * spread(x, i)
        unit = lax.rsqrt(pivots)
        a, x = a * unit, x * unit
        work[low : low + panel, :] = a
        inverse_lower[low : low + panel, :] = x
        if low + panel < width:
            change = lax.dot_general(
                a, jnp.concatenate([a, x], axis=1), (((0,), (0,)), ((), ())),
                precision=lax.Precision.HIGHEST, preferred_element_type=jnp.float32,
            )
            below = low + panel
            work[below:, :] = work[below:, :] - change[below:, :width]
            inverse_lower[below:, :] = inverse_lower[below:, :] - change[below:, width:]

    triangle[...] = jnp.where(row_at <= col_at, work[...], 0.0)
    for h in range(count):
        basis[h] = lax.dot_general(
            sampled[h], inverse_lower[...], (((1,), (1,)), ((), ())),
            precision=lax.Precision.HIGHEST, preferred_element_type=jnp.float32,
        )


def body(walls, harms, sketch, inverse_blocks, couple_up, couple_down, strip_harmonics):
    count, rows, width = sketch.shape
    size = rows * walls
    near = min(4, harms)
    stages = len(bits_of(walls)) + len(bits_of(harms // near)) + near
    gathers = 1 + 2 * SWEEPS
    vmem = pl.BlockSpec(memory_space=pltpu.VMEM)
    anywhere = pl.BlockSpec(memory_space=pl.ANY)
    sampled, gram = pl.pallas_call(
        functools.partial(sweep_kernel, walls, harms),
        out_shape=(
            jax.ShapeDtypeStruct((count, rows, width), jnp.float32),
            jax.ShapeDtypeStruct((width, width), jnp.float32),
        ),
        in_specs=[pl.BlockSpec(memory_space=pltpu.SMEM)] + [anywhere] * 4,
        out_specs=(vmem, vmem),
        scratch_shapes=[
            pltpu.VMEM((gathers, count, size, width), jnp.bfloat16),
            pltpu.VMEM((count, rows, size), jnp.bfloat16),
            pltpu.VMEM((2 * BAND, rows, size), jnp.bfloat16),
            pltpu.VMEM((2 * BAND, count + 2 * BAND, rows, width), jnp.float32),
            pltpu.VMEM((count, rows, width), jnp.float32),
            pltpu.VMEM((SWEEPS, 2, BAND, rows, width), jnp.bfloat16),
            pltpu.VMEM((SWEEPS, 2, BAND, rows, width), jnp.bfloat16),
            pltpu.VMEM((width, width), jnp.float32),
            pltpu.VMEM((width, width), jnp.float32),
            pltpu.VMEM((near, width // 2, width), jnp.float32),
            pltpu.VMEM((stages, width // 2, width), jnp.float32),
            pltpu.VMEM((stages, width // 2, width), jnp.float32),
            pltpu.SemaphoreType.DMA((2 * count + 2,)),
            pltpu.SemaphoreType.DMA((gathers, count, walls)),
            pltpu.SemaphoreType.DMA((count, walls)),
            pltpu.SemaphoreType.DMA((2, BAND)),
            pltpu.SemaphoreType.DMA((SWEEPS, 2, BAND)),
            pltpu.SemaphoreType.DMA((stages,)),
            pltpu.SemaphoreType.DMA((stages,)),
        ],
        compiler_params=pltpu.CompilerParams(
            collective_id=0, has_side_effects=True, vmem_limit_bytes=67043328
        ),
        name="sweeps",
    )(strip_harmonics, sketch, inverse_blocks, couple_up, couple_down)
    return pl.pallas_call(
        factor_kernel,
        out_shape=(
            jax.ShapeDtypeStruct((count, rows, width), jnp.float32),
            jax.ShapeDtypeStruct((width, width), jnp.float32),
        ),
        in_specs=[vmem, vmem],
        out_specs=(vmem, vmem),
        scratch_shapes=[pltpu.VMEM((width, width), jnp.float32)] * 2,
        name="factor",
    )(sampled, gram)


def solution(mesh):
    return jax.shard_map(
        functools.partial(body, mesh.shape["wall"], mesh.shape["harm"]),
        mesh=mesh,
        in_specs=(
            P(("freq", "harm"), "wall", None),
            P(("freq", "harm"), "wall", None),
            P("freq", "wall", None),
            P("freq", "wall", None),
            P("freq"),
        ),
        out_specs=(P(("freq", "harm"), "wall", None), P("freq", None)),
        check_vma=False,
    )
```
